128 devices in a mesh: pipe: 4 (over y), dp: 32 (over x, z, core).
Axes of the slice: x: 4, y: 4, z: 4, core: 2. Of those that a mesh axis runs over, the one named last changes fastest.
Arguments:
- queries: bfloat16 [4, 2, 16384, 4096], P('pipe', None, 'dp'), may hold values from -64 to 64
- keys: bfloat16 [4, 2, 16384, 512], P('pipe', None, 'dp'), may hold values from -6 to 6
- values: bfloat16 [4, 2, 16384, 512], P('pipe', None, 'dp'), may hold values from -6 to 6
- segment: int32 [4, 2, 16384], P('pipe', None, 'dp'), may hold values from 0 to 16383, as said below
- parent: int32 [4, 2, 16384], P('pipe', None, 'dp'), may hold values from 0 to 16382, as said below
- tree_lengths: int32 [4, 2, 128], P('pipe'), may hold values from 0 to 3, as said below
Outputs:
- forward_next: bfloat16 [4, 16384, 4096], P('pipe', 'dp')
- return_next: bfloat16 [4, 16384, 4096], P('pipe', 'dp')
The draws below stay inside these ranges and needn't reach their ends.
Inputs may be any that keep to these rules, and one draw needn't show every extreme that they name: `tree_lengths`: each row lists the trees of one micro-batch in order: entries of 1 to 3 blocks that sum to 128, then zeros; some tree is exactly 3 blocks long. Within a micro-batch a segment is a run of rows, numbered by the index of its first row; every tree's first row opens a new segment, so no segment spans two trees; the last row of every micro-batch opens a segment of its own. The first segment of a tree is its own parent; every other segment's parent is an earlier segment of the same tree whose parent is that first segment; in every micro-batch the last row's parent is the segment opened by the row before it.
All inputs are finite; a program needn't handle non-finite values.
Results may differ from the reference program's by a relative error of at most 0.0036.
Values may be sent and summed in bfloat16 or wider, within the bound.
A program may use at most 192 MiB of HBM per device.

```python
import math
import jax
import jax.numpy as jnp
from jax import lax

BLK = 128
TREE_MOST = 3
KV_HEADS = 4
GROUP = 8
HEAD = 128
PATHS = 2
ROWS = 16384
BLOCKS = 128
N_PIPE = 4


def layout_draw(key):
    block_shape = (N_PIPE, PATHS, BLOCKS)
    row_shape = (N_PIPE, PATHS, ROWS)
    raw = jax.random.randint(jax.random.fold_in(key, 11), block_shape, 1, TREE_MOST + 1, dtype=jnp.int32)
    block_ids = jnp.arange(BLOCKS, dtype=jnp.int32)
    raw = jnp.where(block_ids == 0, TREE_MOST, raw).astype(jnp.int32)
    ends = jnp.cumsum(raw, axis=-1).astype(jnp.int32)
    starts = ends - raw
    lengths = jnp.where(starts < BLOCKS, jnp.minimum(raw, BLOCKS - starts), 0).astype(jnp.int32)
    inside = (starts[..., None, :] <= block_ids[:, None]) & (lengths[..., None, :] > 0)
    tree_first = jnp.max(jnp.where(inside, starts[..., None, :], 0), axis=-1).astype(jnp.int32)
    row_ids = jnp.arange(ROWS, dtype=jnp.int32)
    row_first = (jnp.repeat(tree_first, BLK, axis=-1) * BLK).astype(jnp.int32)
    broken = jax.random.randint(jax.random.fold_in(key, 12), row_shape, 0, 40, dtype=jnp.int32) == 0
    fresh = broken | (row_ids == row_first) | (row_ids >= ROWS - 2)
    opening = lax.cummax(jnp.where(fresh, row_ids, 0).astype(jnp.int32), axis=2)
    segment = opening.astype(jnp.int32)
    root = row_first
    grouping = (jax.random.randint(jax.random.fold_in(key, 13), row_shape, 0, 4, dtype=jnp.int32) == 0) | (row_ids == row_first) | (row_ids == ROWS - 2)
    grouping = grouping & (row_ids != ROWS - 1)
    segment_groups = jnp.take_along_axis(grouping, opening, axis=-1)
    marks = jnp.where(fresh & grouping, segment, -1).astype(jnp.int32)
    latest = lax.cummax(marks, axis=2)
    parent = jnp.where(segment_groups, root, latest).astype(jnp.int32)
    return (lengths, segment, parent)


def score_draw(key):
    key_shape = (N_PIPE, PATHS, ROWS, KV_HEADS, HEAD)
    query_shape = (N_PIPE, PATHS, ROWS, KV_HEADS, GROUP, HEAD)
    key_part = jax.random.fold_in(key, 21)
    query_part = jax.random.fold_in(key, 22)
    keyset = jnp.clip(jax.random.normal(key_part, key_shape, jnp.float32), -6.0, 6.0)
    queryset = jnp.clip(jax.random.normal(query_part, query_shape, jnp.float32), -6.0, 6.0)
    return (queryset.reshape(N_PIPE, PATHS, ROWS, -1), keyset.reshape(N_PIPE, PATHS, ROWS, -1))


def draw_queries(key, part):
    return score_draw(key)[0].astype(jnp.bfloat16)


def draw_keys(key, part):
    return score_draw(key)[1].astype(jnp.bfloat16)


def draw_segment(key, part):
    return layout_draw(key)[1]


def draw_parent(key, part):
    return layout_draw(key)[2]


def draw_tree_lengths(key, part):
    return layout_draw(key)[0]


def block_levels(own_key, dims, cuts, least, largest):
    def one(dim, shards_of):
        heights = jax.random.uniform(jax.random.fold_in(jax.random.fold_in(own_key, 6), dim), (shards_of,), jnp.float32, least / len(cuts), largest / len(cuts))
        return jnp.repeat(jnp.exp(heights), dims[dim] // shards_of).reshape((-1,) + (1,) * (len(dims) - dim - 1))

    gain = one(*cuts[0])
    for cut in cuts[1:]:
        gain = gain * one(*cut)
    return gain


def centred(own_key, shape, deviation, bound, split=(), held_as=jnp.bfloat16):
    values = jax.random.normal(own_key, shape, jnp.float32) * deviation
    if len(split) > 0:
        values = block_levels(own_key, shape, split, -0.22, 0.18) * values
    return jnp.clip(values, min=-bound, max=bound).astype(held_as)


def setup_inputs(seed: int = 0) -> dict:
    streams_of = jax.random.split(jax.random.key(seed), 7)
    queries = draw_queries(jax.random.fold_in(streams_of[6], 71), 0)
    keys = draw_keys(jax.random.fold_in(streams_of[6], 71), 0)
    values = centred(streams_of[2], (N_PIPE, PATHS, ROWS, KV_HEADS * HEAD), 1.0, 6.0, ((0, 4), (2, 32)))
    segment = draw_segment(jax.random.fold_in(streams_of[6], 71), 0)
    parent = draw_parent(jax.random.fold_in(streams_of[6], 71), 0)
    tree_lengths = draw_tree_lengths(jax.random.fold_in(streams_of[6], 71), 0)
    return dict(queries=queries, keys=keys, values=values, segment=segment, parent=parent, tree_lengths=tree_lengths)


NEG = -1e+30

def tree_index(lengths):
    ends = jnp.cumsum(lengths).astype(jnp.int32)
    starts = ends - lengths
    blocks = jnp.arange(lengths.shape[0], dtype=jnp.int32)
    inside = (starts[None, :] <= blocks[:, None]) & (lengths[None, :] > 0)
    return lax.optimization_barrier(jnp.sum(inside.astype(jnp.int32), axis=1)) - 1

def pad_front(array, fill, reach):
    padding = jnp.full((reach,) + array.shape[1:], fill, array.dtype)
    return jnp.concatenate([padding, array], axis=0)

def micro_batch(operands):
    queries, keys, values, segment, parent, lengths = operands
    reach = (TREE_MOST - 1) * BLK
    span = TREE_MOST * BLK
    tree = jnp.repeat(tree_index(lengths), BLK).astype(jnp.int32)
    position = jnp.arange(ROWS, dtype=jnp.int32)
    key_rows = pad_front(keys, 0, reach)
    value_rows = pad_front(values, 0, reach)
    key_tree = pad_front(tree, -2, reach)
    key_pos = pad_front(position, -1, reach)
    key_seg = pad_front(segment, -3, reach)
    key_par = pad_front(parent, -4, reach)
    scale = 1.0 / math.sqrt(HEAD)

    def one_block(index):
        start = (index * BLK).astype(jnp.int32)
        query = lax.dynamic_slice_in_dim(queries, start, BLK, 0).astype(jnp.float32).reshape(BLK, KV_HEADS, GROUP, HEAD)
        keyset = lax.dynamic_slice_in_dim(key_rows, start, span, 0).astype(jnp.float32).reshape(span, KV_HEADS, HEAD)
        valueset = lax.dynamic_slice_in_dim(value_rows, start, span, 0).astype(jnp.float32).reshape(span, KV_HEADS, HEAD)
        query_tree = lax.dynamic_slice_in_dim(tree, start, BLK, 0)
        query_pos = lax.dynamic_slice_in_dim(position, start, BLK, 0)
        query_seg = lax.dynamic_slice_in_dim(segment, start, BLK, 0)
        query_par = lax.dynamic_slice_in_dim(parent, start, BLK, 0)
        window_tree = lax.dynamic_slice_in_dim(key_tree, start, span, 0)
        window_pos = lax.dynamic_slice_in_dim(key_pos, start, span, 0)
        window_seg = lax.dynamic_slice_in_dim(key_seg, start, span, 0)
        window_par = lax.dynamic_slice_in_dim(key_par, start, span, 0)
        related = (window_seg[None, :] == query_seg[:, None]) | (window_seg[None, :] == query_par[:, None]) | (window_par == window_seg)[None, :]
        allowed = (window_tree[None, :] == query_tree[:, None]) & (window_pos[None, :] <= query_pos[:, None]) & related
        scores = jnp.einsum('qhgd,khd->hgqk', query, keyset) * scale
        scores = jnp.where(allowed[None, None], scores, NEG)
        top = lax.optimization_barrier(jnp.max(scores, axis=-1, keepdims=True))
        weights = jnp.exp(scores - top)
        totals = lax.optimization_barrier(jnp.sum(weights, axis=-1))
        rounded = lax.optimization_barrier(weights.astype(jnp.bfloat16)).astype(jnp.float32)
        mixed = jnp.einsum('hgqk,khd->qhgd', rounded, valueset)
        totals = jnp.transpose(totals, (2, 0, 1))[..., None]
        return (mixed / totals).astype(jnp.bfloat16).reshape(BLK, KV_HEADS * GROUP * HEAD)
    result = lax.map(one_block, jnp.arange(BLOCKS, dtype=jnp.int32))
    return result.reshape(ROWS, KV_HEADS * GROUP * HEAD)

def reference(queries, keys, values, segment, parent, tree_lengths):
    count = N_PIPE * PATHS
    operands = (queries.reshape(count, ROWS, -1), keys.reshape(count, ROWS, -1), values.reshape(count, ROWS, -1), segment.reshape(count, ROWS), parent.reshape(count, ROWS), tree_lengths.reshape(count, BLOCKS))
    context = lax.map(micro_batch, operands).reshape(N_PIPE, PATHS, ROWS, -1)
    forward_next = jnp.concatenate([context[0:1, 1], context[:-1, 0]], axis=0)
    return_next = jnp.concatenate([context[1:, 1], context[-1:, 0]], axis=0)
    return (forward_next, return_next)
```

```python
import functools
import math

import jax
import jax.numpy as jnp
from jax import lax
from jax.experimental import pallas as pl
from jax.experimental.pallas import tpu as pltpu
from jax.sharding import PartitionSpec as P

BLK = 128
TREE_MOST = 3
KV_HEADS = 4
GROUP = 8
HEAD = 128
ROWS = 512
BLOCKS = ROWS // BLK
REACH = (TREE_MOST - 1) * BLK
SPAN = TREE_MOST * BLK
WIDE = GROUP * HEAD
STEPS = BLOCKS * KV_HEADS

NEG = -1e30
MESH = pl.DeviceIdType.MESH


def kernel(
    queries, keys, values, segment, parent,
    forward, returned,
    qbuf, kbuf, vbuf, segbuf, parbuf, bias, stage,
    qsem, ownsem, halo_send, halo_recv, send, land_forward, land_returned,
):
    n_pipe, n_dp = lax.axis_size("pipe"), lax.axis_size("dp")
    place, me = lax.axis_index("pipe"), lax.axis_index("dp")
    after, before = lax.rem(me + 1, n_dp), lax.rem(me + n_dp - 1, n_dp)
    up, down = lax.rem(place + 1, n_pipe), lax.rem(place + n_pipe - 1, n_pipe)

    barrier = pltpu.get_barrier_semaphore()
    for target in ((place, after), (place, before), (up, me), (down, me)):
        pl.semaphore_signal(barrier, inc=1, device_id=target, device_id_type=MESH)

    own = [
        pltpu.make_async_copy(source, target, ownsem.at[index])
        for index, (source, target) in enumerate(
            (
                (segment, segbuf.at[:, pl.ds(REACH, ROWS)]),
                (parent, parbuf.at[:, pl.ds(REACH, ROWS)]),
                (keys, kbuf.at[:, pl.ds(REACH, ROWS)]),
                (values, vbuf.at[:, pl.ds(REACH, ROWS)]),
            )
        )
    ]
    for copy in own:
        copy.start()

    def place_of(step):
        block = lax.rem(step // KV_HEADS + (TREE_MOST - 1), BLOCKS)
        head = lax.rem(step, KV_HEADS)
        return (
            block,
            head,
            pl.ds(pl.multiple_of(block * BLK, BLK), BLK),
            pl.ds(pl.multiple_of(head * WIDE, WIDE), WIDE),
        )

    def query_copy(step):
        _, _, rows, columns = place_of(step)
        return pltpu.make_async_copy(
            queries.at[:, rows, columns], qbuf.at[:, rows, columns], qsem.at[step]
        )

    @pl.loop(0, STEPS)
    def _(step):
        query_copy(step).start()

    pl.semaphore_wait(barrier, 4)
    tail = pl.ds(ROWS - REACH, REACH)
    halo = [
        pltpu.make_async_remote_copy(
            src_ref=source,
            dst_ref=target,
            send_sem=halo_send.at[index],
            recv_sem=halo_recv.at[index],
            device_id=(place, after),
            device_id_type=MESH,
        )
        for index, (source, target) in enumerate(
            (
                (segment.at[:, tail], segbuf.at[:, pl.ds(0, REACH)]),
                (parent.at[:, tail], parbuf.at[:, pl.ds(0, REACH)]),
                (keys.at[:, tail], kbuf.at[:, pl.ds(0, REACH)]),
                (values.at[:, tail], vbuf.at[:, pl.ds(0, REACH)]),
            )
        )
    ]
    for copy in halo:
        copy.start()

    def row_of(ref, path, window_block):
        row = ref[path : path + 1, window_block * BLK : (window_block + 1) * BLK]
        return row.astype(jnp.float32)

    def build_bias(path, block):
        later = lax.broadcasted_iota(jnp.int32, (BLK, BLK), 1) <= lax.broadcasted_iota(
            jnp.int32, (BLK, BLK), 0
        )
        segs = [row_of(segbuf, path, block + index) for index in range(TREE_MOST)]
        pars = [row_of(parbuf, path, block + index) for index in range(TREE_MOST)]
        first = jnp.full((1, BLK), -1.0, jnp.float32)
        for index in range(TREE_MOST):
            opening = jnp.where(segs[index] == pars[index], segs[index], -1.0)
            if block + index < TREE_MOST - 1:
                opening = jnp.where(me > 0, opening, -1.0)
            first = jnp.maximum(first, opening)
        root = jnp.broadcast_to(jnp.max(first, axis=1, keepdims=True), (BLK, BLK))
        own_seg = jnp.broadcast_to(segs[-1], (BLK, BLK)).T
        own_par = jnp.broadcast_to(pars[-1], (BLK, BLK)).T
        for index in range(TREE_MOST):
            other = jnp.broadcast_to(segs[index], (BLK, BLK))
            allowed = (other == own_seg) | (other == own_par) | (other == root)
            if index == TREE_MOST - 1:
                allowed = allowed & later
            bias[path * BLOCKS + block, :, index * BLK : (index + 1) * BLK] = jnp.where(
                allowed, 0.0, NEG
            )

    scale = math.log2(math.e) / math.sqrt(HEAD)

    def attend(path, block, head, rows, columns):
        window = pl.ds(pl.multiple_of(block * BLK, BLK), SPAN)
        lanes = pl.ds(pl.multiple_of(head * HEAD, HEAD), HEAD)
        key = kbuf[path, window, lanes]
        value = vbuf[path, window, lanes]
        mask = bias[path * BLOCKS + block]
        for member in range(GROUP):
            part = pl.ds(pl.multiple_of(head * WIDE + member * HEAD, HEAD), HEAD)
            query = qbuf[path, rows, part]
            scores = lax.dot_general(
                query, key, (((1,), (1,)), ((), ())), preferred_element_type=jnp.float32
            )
            scores = scores * scale + mask
            top = jnp.max(scores, axis=1, keepdims=True)
            weights = jnp.exp2(scores - top)
            totals = jnp.sum(weights, axis=1, keepdims=True)
            mixed = jnp.dot(
                weights.astype(jnp.bfloat16), value, preferred_element_type=jnp.float32
            )
            stage[path, rows, part] = (mixed / totals).astype(jnp.bfloat16)

    def away(path, step):
        _, _, rows, columns = place_of(step)
        target, landed, to = (
            (forward, land_forward, up) if path == 0 else (returned, land_returned, down)
        )
        return pltpu.make_async_remote_copy(
            src_ref=stage.at[path, rows, columns],
            dst_ref=target.at[rows, columns],
            send_sem=send.at[path, step],
            recv_sem=landed.at[step],
            device_id=(to, me),
            device_id_type=MESH,
        )

    def stay(path, step):
        _, _, rows, columns = place_of(step)
        target, landed = (
            (returned, land_returned) if path == 0 else (forward, land_forward)
        )
        return pltpu.make_async_copy(
            stage.at[path, rows, columns], target.at[rows, columns], landed.at[step]
        )

    edges = (n_pipe - 1, 0)

    def work(step):
        block, head, rows, columns = place_of(step)
        query_copy(step).wait()
        for path in range(2):
            attend(path, block, head, rows, columns)

            @pl.when(place != edges[path])
            def _():
                away(path, step).start()

            @pl.when(place == edges[path])
            def _():
                stay(path, step).start()

    for copy in own:
        copy.wait()
    for path in range(2):
        for block in range(TREE_MOST - 1, BLOCKS):
            build_bias(path, block)
    half = (BLOCKS - TREE_MOST + 1) * KV_HEADS
    pl.loop(0, half)(work)
    for copy in halo:
        copy.wait()
    for path in range(2):
        for block in range(TREE_MOST - 1):
            build_bias(path, block)
    pl.loop(half, STEPS)(work)

    @pl.loop(0, STEPS)
    def _(step):
        for path in range(2):

            @pl.when(place != edges[path])
            def _():
                away(path, step).wait_send()

            @pl.when(place != edges[1 - path])
            def _():
                away(path, step).wait_recv()

            @pl.when(place == edges[path])
            def _():
                stay(path, step).wait()


def on_device(queries, keys, values, segment, parent, tree_lengths):
    hbm = pl.BlockSpec(memory_space=pl.ANY)
    width = KV_HEADS * GROUP * HEAD
    narrow = KV_HEADS * HEAD
    out = jax.ShapeDtypeStruct((ROWS, width), jnp.bfloat16)
    forward, returned = pl.pallas_call(
        kernel,
        out_shape=(out, out),
        in_specs=[hbm] * 5,
        out_specs=[hbm] * 2,
        scratch_shapes=[
            pltpu.VMEM((2, ROWS, width), jnp.bfloat16),
            pltpu.VMEM((2, REACH + ROWS, narrow), jnp.bfloat16),
            pltpu.VMEM((2, REACH + ROWS, narrow), jnp.bfloat16),
            pltpu.VMEM((2, REACH + ROWS), jnp.int32),
            pltpu.VMEM((2, REACH + ROWS), jnp.int32),
            pltpu.VMEM((2 * BLOCKS, BLK, SPAN), jnp.float32),
            pltpu.VMEM((2, ROWS, width), jnp.bfloat16),
            pltpu.SemaphoreType.DMA((STEPS,)),
            pltpu.SemaphoreType.DMA((4,)),
            pltpu.SemaphoreType.DMA((4,)),
            pltpu.SemaphoreType.DMA((4,)),
            pltpu.SemaphoreType.DMA((2, STEPS)),
            pltpu.SemaphoreType.DMA((STEPS,)),
            pltpu.SemaphoreType.DMA((STEPS,)),
        ],
        compiler_params=pltpu.CompilerParams(
            collective_id=0, has_side_effects=True, vmem_limit_bytes=40 << 20
        ),
        name="relay",
    )(queries[0], keys[0], values[0], segment[0], parent[0])
    return (forward[None], returned[None])


def solution(mesh):
    return jax.shard_map(
        on_device,
        mesh=mesh,
        in_specs=(
            P("pipe", None, "dp", None),
            P("pipe", None, "dp", None),
            P("pipe", None, "dp", None),
            P("pipe", None, "dp"),
            P("pipe", None, "dp"),
            P("pipe", None, None),
        ),
        out_specs=(P("pipe", "dp", None), P("pipe", "dp", None)),
        check_vma=False,
    )
```

```python
import functools
import math

import jax
import jax.numpy as jnp
from jax import lax
from jax.experimental import pallas as pl
from jax.experimental.pallas import tpu as pltpu
from jax.sharding import PartitionSpec as P

BLK = 128
TREE_MOST = 3
KV_HEADS = 4
GROUP = 8
HEAD = 128
ROWS = 512
BLOCKS = ROWS // BLK
REACH = (TREE_MOST - 1) * BLK
SPAN = TREE_MOST * BLK
WIDE = GROUP * HEAD
STEPS = BLOCKS * KV_HEADS
AHEAD = 3

NEG = -1e30
MESH = pl.DeviceIdType.MESH


def kernel(
    queries, keys, values, segment, parent,
    forward, returned,
    qbuf, kbuf, vbuf, segbuf, parbuf, bias, stage,
    qsem, infosem, ownsem, halo_send, halo_recv, send, land_forward, land_returned,
):
    n_pipe, n_dp = lax.axis_size("pipe"), lax.axis_size("dp")
    place, me = lax.axis_index("pipe"), lax.axis_index("dp")
    after, before = lax.rem(me + 1, n_dp), lax.rem(me + n_dp - 1, n_dp)
    up, down = lax.rem(place + 1, n_pipe), lax.rem(place + n_pipe - 1, n_pipe)

    barrier = pltpu.get_barrier_semaphore()
    for target in ((place, after), (place, before), (up, me), (down, me)):
        pl.semaphore_signal(barrier, inc=1, device_id=target, device_id_type=MESH)

    def place_of(step):
        block = lax.rem(step // KV_HEADS + (TREE_MOST - 1), BLOCKS)
        head = lax.rem(step, KV_HEADS)
        return (
            block,
            head,
            pl.ds(pl.multiple_of(block * BLK, BLK), BLK),
            pl.ds(pl.multiple_of(head * WIDE, WIDE), WIDE),
        )

    def query_copy(step):
        _, _, rows, columns = place_of(step)
        return pltpu.make_async_copy(
            queries.at[:, rows, columns], qbuf.at[:, rows, columns], qsem.at[step]
        )

    def own_copy(index, head):
        source, target = ((keys, kbuf), (values, vbuf))[index]
        lanes = pl.ds(head * HEAD, HEAD)
        return pltpu.make_async_copy(
            source.at[:, :, lanes],
            target.at[:, pl.ds(REACH, ROWS), lanes],
            ownsem.at[index, head],
        )

    infos = [
        pltpu.make_async_copy(source, target.at[:, pl.ds(REACH, ROWS)], infosem.at[index])
        for index, (source, target) in enumerate(((segment, segbuf), (parent, parbuf)))
    ]
    for copy in infos:
        copy.start()
    own_copy(0, 0).start()
    query_copy(0).start()
    own_copy(1, 0).start()
    for head in range(1, KV_HEADS):
        own_copy(0, head).start()
        own_copy(1, head).start()
    for step in range(1, AHEAD):
        query_copy(step).start()

    tail = pl.ds(ROWS - REACH, REACH)
    halo = [
        pltpu.make_async_remote_copy(
            src_ref=source.at[:, tail],
            dst_ref=target.at[:, pl.ds(0, REACH)],
            send_sem=halo_send.at[index],
            recv_sem=halo_recv.at[index],
            device_id=(place, after),
            device_id_type=MESH,
        )
        for index, (source, target) in enumerate(
            ((segment, segbuf), (parent, parbuf), (keys, kbuf), (values, vbuf))
        )
    ]

    def row_of(ref, path, window_block):
        row = ref[path : path + 1, window_block * BLK : (window_block + 1) * BLK]
        return row.astype(jnp.float32)

    def build_bias(path, block):
        later = lax.broadcasted_iota(jnp.int32, (BLK, BLK), 1) <= lax.broadcasted_iota(
            jnp.int32, (BLK, BLK), 0
        )
        segs = [row_of(segbuf, path, block + index) for index in range(TREE_MOST)]
        pars = [row_of(parbuf, path, block + index) for index in range(TREE_MOST)]
        first = jnp.full((1, BLK), -1.0, jnp.float32)
        for index in range(TREE_MOST):
            opening = jnp.where(segs[index] == pars[index], segs[index], -1.0)
            if block + index < TREE_MOST - 1:
                opening = jnp.where(me > 0, opening, -1.0)
            first = jnp.maximum(first, opening)
        root = jnp.broadcast_to(jnp.max(first, axis=1, keepdims=True), (BLK, BLK))
        own_seg = jnp.broadcast_to(segs[-1], (BLK, BLK)).T
        own_par = jnp.broadcast_to(pars[-1], (BLK, BLK)).T
        for index in range(TREE_MOST):
            other = jnp.broadcast_to(segs[index], (BLK, BLK))
            allowed = (other == own_seg) | (other == own_par) | (other == root)
            if index == TREE_MOST - 1:
                allowed = allowed & later
            bias[path * BLOCKS + block, :, index * BLK : (index + 1) * BLK] = jnp.where(
                allowed, 0.0, NEG
            )

    scale = math.log2(math.e) / math.sqrt(HEAD)

    def attend(path, step, members):
        block, head, rows, _ = place_of(step)
        window = pl.ds(pl.multiple_of(block * BLK, BLK), SPAN)
        lanes = pl.ds(pl.multiple_of(head * HEAD, HEAD), HEAD)
        key = kbuf[path, window, lanes]
        value = vbuf[path, window, lanes]
        mask = bias[path * BLOCKS + block]
        parts = [
            pl.ds(pl.multiple_of(head * WIDE + member * HEAD, HEAD), HEAD) for member in members
        ]
        query = jnp.concatenate([qbuf[path, rows, part] for part in parts], axis=0)
        scores = lax.dot_general(
            query, key, (((1,), (1,)), ((), ())), preferred_element_type=jnp.float32
        )
        weights, totals = [], []
        for index in range(len(members)):
            score = scores[index * BLK : (index + 1) * BLK] * scale + mask
            weight = jnp.exp2(score - jnp.max(score, axis=1, keepdims=True))
            totals.append(jnp.sum(weight, axis=1, keepdims=True))
            weights.append(weight.astype(jnp.bfloat16))
        mixed = jnp.dot(
            jnp.concatenate(weights, axis=0), value, preferred_element_type=jnp.float32
        )
        for index, part in enumerate(parts):
            result = mixed[index * BLK : (index + 1) * BLK] / totals[index]
            stage[path, rows, part] = result.astype(jnp.bfloat16)

    def region(step, members):
        _, head, rows, _ = place_of(step)
        start = pl.multiple_of(head * WIDE + members[0] * HEAD, HEAD)
        return rows, pl.ds(start, len(members) * HEAD)

    def away(path, step, members):
        rows, columns = region(step, members)
        target, landed, to = (
            (forward, land_forward, up) if path == 0 else (returned, land_returned, down)
        )
        return pltpu.make_async_remote_copy(
            src_ref=stage.at[path, rows, columns],
            dst_ref=target.at[rows, columns],
            send_sem=send.at[path, step],
            recv_sem=landed.at[step],
            device_id=(to, me),
            device_id_type=MESH,
        )

    def stay(path, step, members):
        rows, columns = region(step, members)
        target, landed = (
            (returned, land_returned) if path == 0 else (forward, land_forward)
        )
        return pltpu.make_async_copy(
            stage.at[path, rows, columns], target.at[rows, columns], landed.at[step]
        )

    edges = (n_pipe - 1, 0)
    every = tuple(range(GROUP))

    def leave(path, step, members):
        @pl.when(place != edges[path])
        def _():
            away(path, step, members).start()

        @pl.when(place == edges[path])
        def _():
            stay(path, step, members).start()

    def fetch(step):
        @pl.when(step + AHEAD < STEPS)
        def _():
            query_copy(step + AHEAD).start()

        query_copy(step).wait()

    def work(step):
        fetch(step)
        for path in range(2):
            attend(path, step, every)
            leave(path, step, every)

    for copy in infos:
        copy.wait()
    for path in range(2):
        build_bias(path, TREE_MOST - 1)
    pl.semaphore_wait(barrier, 4)
    for copy in halo:
        copy.start()
    own_copy(0, 0).wait()
    own_copy(1, 0).wait()
    fetch(0)
    for members in ((0,), (1,), (2, 3), (4, 5, 6, 7)):
        for path in range(2):
            attend(path, 0, members)
        for path in range(2):
            leave(path, 0, members)
    for head in range(1, KV_HEADS):
        own_copy(0, head).wait()
        own_copy(1, head).wait()
    pl.loop(1, KV_HEADS)(work)
    for block in range(TREE_MOST, BLOCKS):
        for path in range(2):
            build_bias(path, block)
    half = (BLOCKS - TREE_MOST + 1) * KV_HEADS
    pl.loop(KV_HEADS, half)(work)
    for copy in halo:
        copy.wait()
    for block in range(TREE_MOST - 1):
        for path in range(2):
            build_bias(path, block)
    pl.loop(half, STEPS)(work)

    @pl.loop(0, STEPS)
    def _(step):
        for path in range(2):

            @pl.when(place != edges[path])
            def _():
                away(path, step, every).wait_send()

            @pl.when(place != edges[1 - path])
            def _():
                away(path, step, every).wait_recv()

            @pl.when(place == edges[path])
            def _():
                stay(path, step, every).wait()


def on_device(queries, keys, values, segment, parent, tree_lengths):
    width = KV_HEADS * GROUP * HEAD
    narrow = KV_HEADS * HEAD
    out = jax.ShapeDtypeStruct((ROWS, width), jnp.bfloat16)
    forward, returned = pl.pallas_call(
        kernel,
        out_shape=(out, out),
        in_specs=[pl.BlockSpec(memory_space=pltpu.HBM)] * 5,
        out_specs=[pl.BlockSpec(memory_space=pl.ANY)] * 2,
        scratch_shapes=[
            pltpu.VMEM((2, ROWS, width), jnp.bfloat16),
            pltpu.VMEM((2, REACH + ROWS, narrow), jnp.bfloat16),
            pltpu.VMEM((2, REACH + ROWS, narrow), jnp.bfloat16),
            pltpu.VMEM((2, REACH + ROWS), jnp.int32),
            pltpu.VMEM((2, REACH + ROWS), jnp.int32),
            pltpu.VMEM((2 * BLOCKS, BLK, SPAN), jnp.float32),
            pltpu.VMEM((2, ROWS, width), jnp.bfloat16),
            pltpu.SemaphoreType.DMA((STEPS,)),
            pltpu.SemaphoreType.DMA((2,)),
            pltpu.SemaphoreType.DMA((2, KV_HEADS)),
            pltpu.SemaphoreType.DMA((4,)),
            pltpu.SemaphoreType.DMA((4,)),
            pltpu.SemaphoreType.DMA((2, STEPS)),
            pltpu.SemaphoreType.DMA((STEPS,)),
            pltpu.SemaphoreType.DMA((STEPS,)),
        ],
        compiler_params=pltpu.CompilerParams(
            collective_id=0, has_side_effects=True, vmem_limit_bytes=40 << 20
        ),
        name="relay",
    )(*[pltpu.with_memory_space_constraint(x[0], pltpu.HBM) for x in (queries, keys, values, segment, parent)])
    return (forward[None], returned[None])


def solution(mesh):
    return jax.shard_map(
        on_device,
        mesh=mesh,
        in_specs=(
            P("pipe", None, "dp", None),
            P("pipe", None, "dp", None),
            P("pipe", None, "dp", None),
            P("pipe", None, "dp"),
            P("pipe", None, "dp"),
            P("pipe", None, None),
        ),
        out_specs=(P("pipe", "dp", None), P("pipe", "dp", None)),
        check_vma=False,
    )
```

```python
import functools
import math

import jax
import jax.numpy as jnp
from jax import lax
from jax.experimental import pallas as pl
from jax.experimental.pallas import tpu as pltpu
from jax.sharding import PartitionSpec as P

BLK = 128
TREE_MOST = 3
KV_HEADS = 4
GROUP = 8
HEAD = 128
ROWS = 512
BLOCKS = ROWS // BLK
REACH = (TREE_MOST - 1) * BLK
SPAN = TREE_MOST * BLK
WIDE = GROUP * HEAD
STEPS = BLOCKS * KV_HEADS
AHEAD = 3
PIECES = 2

NEG = -1e30
MESH = pl.DeviceIdType.MESH


def kernel(
    queries, keys, values, segment, parent,
    forward, returned,
    qbuf, kbuf, vbuf, segbuf, parbuf, bias, stage,
    qsem, infosem, ownsem, halo_send, halo_recv, send, land_forward, land_returned,
):
    n_pipe, n_dp = lax.axis_size("pipe"), lax.axis_size("dp")
    place, me = lax.axis_index("pipe"), lax.axis_index("dp")
    after, before = lax.rem(me + 1, n_dp), lax.rem(me + n_dp - 1, n_dp)
    up, down = lax.rem(place + 1, n_pipe), lax.rem(place + n_pipe - 1, n_pipe)

    def place_of(step):
        block = lax.rem(step // KV_HEADS + (TREE_MOST - 1), BLOCKS)
        head = lax.rem(step, KV_HEADS)
        return (
            block,
            head,
            pl.ds(pl.multiple_of(block * BLK, BLK), BLK),
            pl.ds(pl.multiple_of(head * WIDE, WIDE), WIDE),
        )

    def query_copy(step):
        _, _, rows, columns = place_of(step)
        return pltpu.make_async_copy(
            queries.at[:, rows, columns], qbuf.at[:, rows, columns], qsem.at[step]
        )

    def own_copy(index, head):
        source, target = ((keys, kbuf), (values, vbuf))[index]
        lanes = pl.ds(head * HEAD, HEAD)
        return pltpu.make_async_copy(
            source.at[:, :, lanes],
            target.at[:, pl.ds(REACH, ROWS), lanes],
            ownsem.at[index, head],
        )

    infos = [
        pltpu.make_async_copy(source, target.at[:, pl.ds(REACH, ROWS)], infosem.at[index])
        for index, (source, target) in enumerate(((segment, segbuf), (parent, parbuf)))
    ]
    tail = pl.ds(ROWS - REACH, REACH)
    halo = [
        pltpu.make_async_remote_copy(
            src_ref=source.at[:, tail],
            dst_ref=target.at[:, pl.ds(0, REACH)],
            send_sem=halo_send.at[index],
            recv_sem=halo_recv.at[index],
            device_id=(place, after),
            device_id_type=MESH,
        )
        for index, (source, target) in enumerate(
            ((segment, segbuf), (parent, parbuf), (keys, kbuf), (values, vbuf))
        )
    ]

    def row_of(ref, path, window_block):
        row = ref[path : path + 1, window_block * BLK : (window_block + 1) * BLK]
        return row.astype(jnp.float32)

    def build_bias(path, block):
        later = lax.broadcasted_iota(jnp.int32, (BLK, BLK), 1) <= lax.broadcasted_iota(
            jnp.int32, (BLK, BLK), 0
        )
        segs = [row_of(segbuf, path, block + index) for index in range(TREE_MOST)]
        pars = [row_of(parbuf, path, block + index) for index in range(TREE_MOST)]
        first = jnp.full((1, BLK), -1.0, jnp.float32)
        for index in range(TREE_MOST):
            opening = jnp.where(segs[index] == pars[index], segs[index], -1.0)
            if block + index < TREE_MOST - 1:
                opening = jnp.where(me > 0, opening, -1.0)
            first = jnp.maximum(first, opening)
        root = jnp.broadcast_to(jnp.max(first, axis=1, keepdims=True), (BLK, BLK))
        own_seg = jnp.broadcast_to(segs[-1], (BLK, BLK)).T
        own_par = jnp.broadcast_to(pars[-1], (BLK, BLK)).T
        for index in range(TREE_MOST):
            other = jnp.broadcast_to(segs[index], (BLK, BLK))
            allowed = (other == own_seg) | (other == own_par) | (other == root)
            if index == TREE_MOST - 1:
                allowed = allowed & later
            bias[path * BLOCKS + block, :, index * BLK : (index + 1) * BLK] = jnp.where(
                allowed, 0.0, NEG
            )

    scale = math.log2(math.e) / math.sqrt(HEAD)

    def attend(path, step, members):
        block, head, rows, _ = place_of(step)
        window = pl.ds(pl.multiple_of(block * BLK, BLK), SPAN)
        lanes = pl.ds(pl.multiple_of(head * HEAD, HEAD), HEAD)
        key = kbuf[path, window, lanes]
        value = vbuf[path, window, lanes]
        mask = bias[path * BLOCKS + block]
        parts = [
            pl.ds(pl.multiple_of(head * WIDE + member * HEAD, HEAD), HEAD) for member in members
        ]
        query = jnp.concatenate([qbuf[path, rows, part] for part in parts], axis=0)
        scores = lax.dot_general(
            query, key, (((1,), (1,)), ((), ())), preferred_element_type=jnp.float32
        )
        weights, totals = [], []
        for index in range(len(members)):
            score = scores[index * BLK : (index + 1) * BLK] * scale + mask
            weight = jnp.exp2(score - jnp.max(score, axis=1, keepdims=True))
            totals.append(jnp.sum(weight, axis=1, keepdims=True))
            weights.append(weight.astype(jnp.bfloat16))
        mixed = jnp.dot(
            jnp.concatenate(weights, axis=0), value, preferred_element_type=jnp.float32
        )
        for index, part in enumerate(parts):
            result = mixed[index * BLK : (index + 1) * BLK] / totals[index]
            stage[path, rows, part] = result.astype(jnp.bfloat16)

    def region(step, members):
        _, head, rows, _ = place_of(step)
        if members is None:
            return rows, slice(None)
        start = pl.multiple_of(head * WIDE + members[0] * HEAD, HEAD)
        return rows, pl.ds(start, len(members) * HEAD)

    def away(path, step, members):
        rows, columns = region(step, members)
        target, landed, to = (
            (forward, land_forward, up) if path == 0 else (returned, land_returned, down)
        )
        return pltpu.make_async_remote_copy(
            src_ref=stage.at[path, rows, columns],
            dst_ref=target.at[rows, columns],
            send_sem=send.at[path, step],
            recv_sem=landed.at[step],
            device_id=(to, me),
            device_id_type=MESH,
        )

    def stay(path, step, members):
        rows, columns = region(step, members)
        target, landed = (
            (returned, land_returned) if path == 0 else (forward, land_forward)
        )
        return pltpu.make_async_copy(
            stage.at[path, rows, columns], target.at[rows, columns], landed.at[step]
        )

    edges = (n_pipe - 1, 0)
    every = tuple(range(GROUP))

    def leave(path, step, members):
        @pl.when(place != edges[path])
        def _():
            away(path, step, members).start()

        @pl.when(place == edges[path])
        def _():
            stay(path, step, members).start()

    def fetch(step):
        @pl.when(step + AHEAD < STEPS)
        def _():
            query_copy(step + AHEAD).start()

        query_copy(step).wait()

    def work(step):
        fetch(step)
        for path in range(2):
            attend(path, step, every)

            @pl.when(step < KV_HEADS)
            def _():
                leave(path, step, every)

            @pl.when((step >= KV_HEADS) & (lax.rem(step, KV_HEADS) == KV_HEADS - 1))
            def _():
                leave(path, step, None)

    barrier = pltpu.get_barrier_semaphore()
    for target in ((up, me), (down, me), (place, before)):
        pl.semaphore_signal(barrier, inc=1, device_id=target, device_id_type=MESH)
    own_copy(0, 0).start()
    query_copy(0).start()
    for copy in infos:
        copy.start()
    own_copy(1, 0).start()
    own_copy(0, 0).wait()
    query_copy(0).wait()
    for copy in infos:
        copy.wait()
    own_copy(1, 0).wait()
    for path in range(2):
        build_bias(path, TREE_MOST - 1)
    for members in ((0,), (1,), (2, 3), (4, 5, 6, 7)):
        for path in range(2):
            attend(path, 0, members)
        if members == (0,):
            pl.semaphore_wait(barrier, 3)
        for path in range(2):
            leave(path, 0, members)
        if members == (0,):
            for head in range(1, KV_HEADS):
                own_copy(0, head).start()
                own_copy(1, head).start()
            for step in range(1, AHEAD + 1):
                query_copy(step).start()
    for copy in halo:
        copy.start()
    for head in range(1, KV_HEADS):
        own_copy(0, head).wait()
        own_copy(1, head).wait()
    pl.loop(1, KV_HEADS)(work)
    for block in range(TREE_MOST, BLOCKS):
        for path in range(2):
            build_bias(path, block)
    half = (BLOCKS - TREE_MOST + 1) * KV_HEADS
    pl.loop(KV_HEADS, half)(work)
    for copy in halo:
        copy.wait()
    for block in range(TREE_MOST - 1):
        for path in range(2):
            build_bias(path, block)
    pl.loop(half, STEPS)(work)

    def settle(step, members):
        for path in range(2):

            @pl.when(place != edges[path])
            def _():
                away(path, step, members).wait_send()

            @pl.when(place != edges[1 - path])
            def _():
                away(path, step, members).wait_recv()

            @pl.when(place == edges[path])
            def _():
                stay(path, step, members).wait()

    @pl.loop(0, KV_HEADS)
    def _(step):
        settle(step, every)

    @pl.loop(1, BLOCKS)
    def _(block):
        settle(block * KV_HEADS + KV_HEADS - 1, None)


def flush(forward, returned, forward_out, returned_out, sem):
    copies = []
    for source, target in ((forward, forward_out), (returned, returned_out)):
        for index in range(PIECES):
            rows = pl.ds(index * (ROWS // PIECES), ROWS // PIECES)
            copies.append(
                pltpu.make_async_copy(source.at[rows], target.at[rows], sem.at[len(copies)])
            )
    for copy in copies:
        copy.start()
    for copy in copies:
        copy.wait()


def on_device(queries, keys, values, segment, parent, tree_lengths):
    width = KV_HEADS * GROUP * HEAD
    narrow = KV_HEADS * HEAD
    out = jax.ShapeDtypeStruct((ROWS, width), jnp.bfloat16)
    forward, returned = pl.pallas_call(
        kernel,
        out_shape=(out, out),
        in_specs=[pl.BlockSpec(memory_space=pltpu.HBM)] * 5,
        out_specs=[pl.BlockSpec(memory_space=pl.ANY)] * 2,
        scratch_shapes=[
            pltpu.VMEM((2, ROWS, width), jnp.bfloat16),
            pltpu.VMEM((2, REACH + ROWS, narrow), jnp.bfloat16),
            pltpu.VMEM((2, REACH + ROWS, narrow), jnp.bfloat16),
            pltpu.VMEM((2, REACH + ROWS), jnp.int32),
            pltpu.VMEM((2, REACH + ROWS), jnp.int32),
            pltpu.VMEM((2 * BLOCKS, BLK, SPAN), jnp.float32),
            pltpu.VMEM((2, ROWS, width), jnp.bfloat16),
            pltpu.SemaphoreType.DMA((STEPS,)),
            pltpu.SemaphoreType.DMA((2,)),
            pltpu.SemaphoreType.DMA((2, KV_HEADS)),
            pltpu.SemaphoreType.DMA((4,)),
            pltpu.SemaphoreType.DMA((4,)),
            pltpu.SemaphoreType.DMA((2, STEPS)),
            pltpu.SemaphoreType.DMA((STEPS,)),
            pltpu.SemaphoreType.DMA((STEPS,)),
        ],
        compiler_params=pltpu.CompilerParams(
            collective_id=0, has_side_effects=True, vmem_limit_bytes=40 << 20
        ),
        name="relay",
    )(*[pltpu.with_memory_space_constraint(x[0], pltpu.HBM) for x in (queries, keys, values, segment, parent)])
    anywhere = [pl.BlockSpec(memory_space=pl.ANY)] * 2
    forward, returned = pl.pallas_call(
        flush,
        out_shape=(out, out),
        in_specs=anywhere,
        out_specs=anywhere,
        scratch_shapes=[pltpu.SemaphoreType.DMA((2 * PIECES,))],
        compiler_params=pltpu.CompilerParams(vmem_limit_bytes=1 << 20),
        name="flush",
    )(forward, returned)
    return (forward[None], returned[None])


def solution(mesh):
    return jax.shard_map(
        on_device,
        mesh=mesh,
        in_specs=(
            P("pipe", None, "dp", None),
            P("pipe", None, "dp", None),
            P("pipe", None, "dp", None),
            P("pipe", None, "dp"),
            P("pipe", None, "dp"),
            P("pipe", None, None),
        ),
        out_specs=(P("pipe", "dp", None), P("pipe", "dp", None)),
        check_vma=False,
    )
```

```python
import functools
import math

import jax
import jax.numpy as jnp
from jax import lax
from jax.experimental import pallas as pl
from jax.experimental.pallas import tpu as pltpu
from jax.sharding import PartitionSpec as P

BLK = 128
TREE_MOST = 3
KV_HEADS = 4
GROUP = 8
HEAD = 128
ROWS = 512
BLOCKS = ROWS // BLK
REACH = (TREE_MOST - 1) * BLK
SPAN = TREE_MOST * BLK
WIDE = GROUP * HEAD
STEPS = BLOCKS * KV_HEADS
AHEAD = 3
PIECES = 2

NEG = -1e30
MESH = pl.DeviceIdType.MESH


def kernel(
    queries, keys, values, segment, parent,
    forward, returned,
    qbuf, kbuf, vbuf, segbuf, parbuf, bias, stage,
    qsem, headsem, infosem, ownsem, halo_send, halo_recv, send, land_forward, land_returned,
):
    n_pipe, n_dp = lax.axis_size("pipe"), lax.axis_size("dp")
    place, me = lax.axis_index("pipe"), lax.axis_index("dp")
    after, before = lax.rem(me + 1, n_dp), lax.rem(me + n_dp - 1, n_dp)
    up, down = lax.rem(place + 1, n_pipe), lax.rem(place + n_pipe - 1, n_pipe)

    def place_of(step):
        block = lax.rem(step // KV_HEADS + (TREE_MOST - 1), BLOCKS)
        head = lax.rem(step, KV_HEADS)
        return (
            block,
            head,
            pl.ds(pl.multiple_of(block * BLK, BLK), BLK),
            pl.ds(pl.multiple_of(head * WIDE, WIDE), WIDE),
        )

    def query_copy(step):
        _, _, rows, columns = place_of(step)
        return pltpu.make_async_copy(
            queries.at[:, rows, columns], qbuf.at[:, rows, columns], qsem.at[step]
        )

    def own_copy(index, head):
        source, target = ((keys, kbuf), (values, vbuf))[index]
        lanes = pl.ds(head * HEAD, HEAD)
        return pltpu.make_async_copy(
            source.at[:, :, lanes],
            target.at[:, pl.ds(REACH, ROWS), lanes],
            ownsem.at[index, head],
        )

    infos = [
        pltpu.make_async_copy(source, target.at[:, pl.ds(REACH, ROWS)], infosem.at[index])
        for index, (source, target) in enumerate(((segment, segbuf), (parent, parbuf)))
    ]
    tail = pl.ds(ROWS - REACH, REACH)
    halo = [
        pltpu.make_async_remote_copy(
            src_ref=source.at[:, tail],
            dst_ref=target.at[:, pl.ds(0, REACH)],
            send_sem=halo_send.at[index],
            recv_sem=halo_recv.at[index],
            device_id=(place, after),
            device_id_type=MESH,
        )
        for index, (source, target) in enumerate(
            ((segment, segbuf), (parent, parbuf), (keys, kbuf), (values, vbuf))
        )
    ]

    def row_of(ref, path, window_block):
        row = ref[path : path + 1, window_block * BLK : (window_block + 1) * BLK]
        return row.astype(jnp.float32)

    def build_bias(path, block):
        later = lax.broadcasted_iota(jnp.int32, (BLK, BLK), 1) <= lax.broadcasted_iota(
            jnp.int32, (BLK, BLK), 0
        )
        segs = [row_of(segbuf, path, block + index) for index in range(TREE_MOST)]
        pars = [row_of(parbuf, path, block + index) for index in range(TREE_MOST)]
        first = jnp.full((1, BLK), -1.0, jnp.float32)
        for index in range(TREE_MOST):
            opening = jnp.where(segs[index] == pars[index], segs[index], -1.0)
            if block + index < TREE_MOST - 1:
                opening = jnp.where(me > 0, opening, -1.0)
            first = jnp.maximum(first, opening)
        root = jnp.broadcast_to(jnp.max(first, axis=1, keepdims=True), (BLK, BLK))
        own_seg = jnp.broadcast_to(segs[-1], (BLK, BLK)).T
        own_par = jnp.broadcast_to(pars[-1], (BLK, BLK)).T
        for index in range(TREE_MOST):
            other = jnp.broadcast_to(segs[index], (BLK, BLK))
            allowed = (other == own_seg) | (other == own_par) | (other == root)
            if index == TREE_MOST - 1:
                allowed = allowed & later
            bias[path * BLOCKS + block, :, index * BLK : (index + 1) * BLK] = jnp.where(
                allowed, 0.0, NEG
            )

    scale = math.log2(math.e) / math.sqrt(HEAD)

    def attend(path, step, members):
        block, head, rows, _ = place_of(step)
        window = pl.ds(pl.multiple_of(block * BLK, BLK), SPAN)
        lanes = pl.ds(pl.multiple_of(head * HEAD, HEAD), HEAD)
        key = kbuf[path, window, lanes]
        value = vbuf[path, window, lanes]
        mask = bias[path * BLOCKS + block]
        parts = [
            pl.ds(pl.multiple_of(head * WIDE + member * HEAD, HEAD), HEAD) for member in members
        ]
        query = jnp.concatenate([qbuf[path, rows, part] for part in parts], axis=0)
        scores = lax.dot_general(
            query, key, (((1,), (1,)), ((), ())), preferred_element_type=jnp.float32
        )
        weights, totals = [], []
        for index in range(len(members)):
            score = scores[index * BLK : (index + 1) * BLK] * scale + mask
            weight = jnp.exp2(score - jnp.max(score, axis=1, keepdims=True))
            totals.append(jnp.sum(weight, axis=1, keepdims=True))
            weights.append(weight.astype(jnp.bfloat16))
        mixed = jnp.dot(
            jnp.concatenate(weights, axis=0), value, preferred_element_type=jnp.float32
        )
        for index, part in enumerate(parts):
            result = mixed[index * BLK : (index + 1) * BLK] / totals[index]
            stage[path, rows, part] = result.astype(jnp.bfloat16)

    def region(step, members):
        _, head, rows, _ = place_of(step)
        if members is None:
            return rows, slice(None)
        start = pl.multiple_of(head * WIDE + members[0] * HEAD, HEAD)
        return rows, pl.ds(start, len(members) * HEAD)

    def away(path, step, members):
        rows, columns = region(step, members)
        target, landed, to = (
            (forward, land_forward, up) if path == 0 else (returned, land_returned, down)
        )
        return pltpu.make_async_remote_copy(
            src_ref=stage.at[path, rows, columns],
            dst_ref=target.at[rows, columns],
            send_sem=send.at[path, step],
            recv_sem=landed.at[step],
            device_id=(to, me),
            device_id_type=MESH,
        )

    def stay(path, step, members):
        rows, columns = region(step, members)
        target, landed = (
            (returned, land_returned) if path == 0 else (forward, land_forward)
        )
        return pltpu.make_async_copy(
            stage.at[path, rows, columns], target.at[rows, columns], landed.at[step]
        )

    edges = (n_pipe - 1, 0)
    every = tuple(range(GROUP))

    def leave(path, step, members):
        @pl.when(place != edges[path])
        def _():
            away(path, step, members).start()

        @pl.when(place == edges[path])
        def _():
            stay(path, step, members).start()

    def fetch(step):
        @pl.when(step + AHEAD < STEPS)
        def _():
            query_copy(step + AHEAD).start()

        query_copy(step).wait()

    def work(step):
        fetch(step)
        for path in range(2):
            attend(path, step, every)

            @pl.when(step < KV_HEADS)
            def _():
                leave(path, step, every)

            @pl.when((step >= KV_HEADS) & (lax.rem(step, KV_HEADS) == KV_HEADS - 1))
            def _():
                leave(path, step, None)

    barrier = pltpu.get_barrier_semaphore()
    for target in ((up, me), (down, me), (place, before)):
        pl.semaphore_signal(barrier, inc=1, device_id=target, device_id_type=MESH)
    opening_rows = pl.ds((TREE_MOST - 1) * BLK, BLK)
    heads = [
        pltpu.make_async_copy(
            queries.at[:, opening_rows, lanes], qbuf.at[:, opening_rows, lanes], headsem.at[index]
        )
        for index, lanes in enumerate((pl.ds(0, HEAD), pl.ds(HEAD, WIDE - HEAD)))
    ]
    for copy in infos:
        copy.start()
    own_copy(0, 0).start()
    heads[0].start()
    own_copy(1, 0).start()
    heads[1].start()
    own_copy(0, 0).wait()
    heads[0].wait()
    for copy in infos:
        copy.wait()
    own_copy(1, 0).wait()
    for path in range(2):
        build_bias(path, TREE_MOST - 1)
    for members in ((0,), (1,), (2,), (3, 4), (5, 6, 7)):
        for path in range(2):
            attend(path, 0, members)
        if members == (0,):
            pl.semaphore_wait(barrier, 3)
        for path in range(2):
            leave(path, 0, members)
        if members == (0,):
            for head in range(1, KV_HEADS):
                own_copy(0, head).start()
                own_copy(1, head).start()
            for step in range(1, AHEAD + 1):
                query_copy(step).start()
            heads[1].wait()
    for copy in halo:
        copy.start()
    for head in range(1, KV_HEADS):
        own_copy(0, head).wait()
        own_copy(1, head).wait()
    pl.loop(1, KV_HEADS)(work)
    for block in range(TREE_MOST, BLOCKS):
        for path in range(2):
            build_bias(path, block)
    half = (BLOCKS - TREE_MOST + 1) * KV_HEADS
    pl.loop(KV_HEADS, half)(work)
    for copy in halo:
        copy.wait()
    for block in range(TREE_MOST - 1):
        for path in range(2):
            build_bias(path, block)
    pl.loop(half, STEPS)(work)

    def settle(step, members):
        for path in range(2):

            @pl.when(place != edges[path])
            def _():
                away(path, step, members).wait_send()

            @pl.when(place != edges[1 - path])
            def _():
                away(path, step, members).wait_recv()

            @pl.when(place == edges[path])
            def _():
                stay(path, step, members).wait()

    @pl.loop(0, KV_HEADS)
    def _(step):
        settle(step, every)

    @pl.loop(1, BLOCKS)
    def _(block):
        settle(block * KV_HEADS + KV_HEADS - 1, None)


def flush(forward, returned, forward_out, returned_out, sem):
    copies = []
    for source, target in ((forward, forward_out), (returned, returned_out)):
        for index in range(PIECES):
            rows = pl.ds(index * (ROWS // PIECES), ROWS // PIECES)
            copies.append(
                pltpu.make_async_copy(source.at[rows], target.at[rows], sem.at[len(copies)])
            )
    for copy in copies:
        copy.start()
    for copy in copies:
        copy.wait()


def on_device(queries, keys, values, segment, parent, tree_lengths):
    width = KV_HEADS * GROUP * HEAD
    narrow = KV_HEADS * HEAD
    out = jax.ShapeDtypeStruct((ROWS, width), jnp.bfloat16)
    forward, returned = pl.pallas_call(
        kernel,
        out_shape=(out, out),
        in_specs=[pl.BlockSpec(memory_space=pltpu.HBM)] * 5,
        out_specs=[pl.BlockSpec(memory_space=pl.ANY)] * 2,
        scratch_shapes=[
            pltpu.VMEM((2, ROWS, width), jnp.bfloat16),
            pltpu.VMEM((2, REACH + ROWS, narrow), jnp.bfloat16),
            pltpu.VMEM((2, REACH + ROWS, narrow), jnp.bfloat16),
            pltpu.VMEM((2, REACH + ROWS), jnp.int32),
            pltpu.VMEM((2, REACH + ROWS), jnp.int32),
            pltpu.VMEM((2 * BLOCKS, BLK, SPAN), jnp.float32),
            pltpu.VMEM((2, ROWS, width), jnp.bfloat16),
            pltpu.SemaphoreType.DMA((STEPS,)),
            pltpu.SemaphoreType.DMA((2,)),
            pltpu.SemaphoreType.DMA((2,)),
            pltpu.SemaphoreType.DMA((2, KV_HEADS)),
            pltpu.SemaphoreType.DMA((4,)),
            pltpu.SemaphoreType.DMA((4,)),
            pltpu.SemaphoreType.DMA((2, STEPS)),
            pltpu.SemaphoreType.DMA((STEPS,)),
            pltpu.SemaphoreType.DMA((STEPS,)),
        ],
        compiler_params=pltpu.CompilerParams(
            collective_id=0, has_side_effects=True, vmem_limit_bytes=40 << 20
        ),
        name="relay",
    )(*[pltpu.with_memory_space_constraint(x[0], pltpu.HBM) for x in (queries, keys, values, segment, parent)])
    anywhere = [pl.BlockSpec(memory_space=pl.ANY)] * 2
    forward, returned = pl.pallas_call(
        flush,
        out_shape=(out, out),
        in_specs=anywhere,
        out_specs=anywhere,
        scratch_shapes=[pltpu.SemaphoreType.DMA((2 * PIECES,))],
        compiler_params=pltpu.CompilerParams(vmem_limit_bytes=1 << 20),
        name="flush",
    )(forward, returned)
    return (forward[None], returned[None])


def solution(mesh):
    return jax.shard_map(
        on_device,
        mesh=mesh,
        in_specs=(
            P("pipe", None, "dp", None),
            P("pipe", None, "dp", None),
            P("pipe", None, "dp", None),
            P("pipe", None, "dp"),
            P("pipe", None, "dp"),
            P("pipe", None, None),
        ),
        out_specs=(P("pipe", "dp", None), P("pipe", "dp", None)),
        check_vma=False,
    )
```

```python
import functools
import math

import jax
import jax.numpy as jnp
from jax import lax
from jax.experimental import pallas as pl
from jax.experimental.pallas import tpu as pltpu
from jax.sharding import PartitionSpec as P

BLK = 128
TREE_MOST = 3
KV_HEADS = 4
GROUP = 8
HEAD = 128
ROWS = 512
BLOCKS = ROWS // BLK
REACH = (TREE_MOST - 1) * BLK
SPAN = TREE_MOST * BLK
WIDE = GROUP * HEAD
STEPS = BLOCKS * KV_HEADS
AHEAD = 3
PIECES = 2

NEG = -1e30
MESH = pl.DeviceIdType.MESH


def kernel(
    queries, keys, values, segment, parent,
    forward, returned,
    qbuf, kbuf, vbuf, segbuf, parbuf, bias, stage,
    qsem, infosem, ownsem, halo_send, halo_recv, send, land_forward, land_returned,
):
    n_pipe, n_dp = lax.axis_size("pipe"), lax.axis_size("dp")
    place, me = lax.axis_index("pipe"), lax.axis_index("dp")
    after, before = lax.rem(me + 1, n_dp), lax.rem(me + n_dp - 1, n_dp)
    up, down = lax.rem(place + 1, n_pipe), lax.rem(place + n_pipe - 1, n_pipe)

    def place_of(step):
        block = lax.rem(step // KV_HEADS + (TREE_MOST - 1), BLOCKS)
        head = lax.rem(step, KV_HEADS)
        return (
            block,
            head,
            pl.ds(pl.multiple_of(block * BLK, BLK), BLK),
            pl.ds(pl.multiple_of(head * WIDE, WIDE), WIDE),
        )

    def query_copy(step):
        _, _, rows, columns = place_of(step)
        return pltpu.make_async_copy(
            queries.at[:, rows, columns], qbuf.at[:, rows, columns], qsem.at[step]
        )

    def own_copy(index, head):
        source, target = ((keys, kbuf), (values, vbuf))[index]
        lanes = pl.ds(head * HEAD, HEAD)
        return pltpu.make_async_copy(
            source.at[:, :, lanes],
            target.at[:, pl.ds(REACH, ROWS), lanes],
            ownsem.at[index, head],
        )

    infos = [
        pltpu.make_async_copy(source, target.at[:, pl.ds(REACH, ROWS)], infosem.at[index])
        for index, (source, target) in enumerate(((segment, segbuf), (parent, parbuf)))
    ]
    tail = pl.ds(ROWS - REACH, REACH)
    halo = [
        pltpu.make_async_remote_copy(
            src_ref=source.at[:, tail],
            dst_ref=target.at[:, pl.ds(0, REACH)],
            send_sem=halo_send.at[index],
            recv_sem=halo_recv.at[index],
            device_id=(place, after),
            device_id_type=MESH,
        )
        for index, (source, target) in enumerate(
            ((segment, segbuf), (parent, parbuf), (keys, kbuf), (values, vbuf))
        )
    ]

    def row_of(ref, path, window_block):
        row = ref[path : path + 1, window_block * BLK : (window_block + 1) * BLK]
        return row.astype(jnp.float32)

    def build_bias(path, block):
        later = lax.broadcasted_iota(jnp.int32, (BLK, BLK), 1) <= lax.broadcasted_iota(
            jnp.int32, (BLK, BLK), 0
        )
        segs = [row_of(segbuf, path, block + index) for index in range(TREE_MOST)]
        pars = [row_of(parbuf, path, block + index) for index in range(TREE_MOST)]
        first = jnp.full((1, BLK), -1.0, jnp.float32)
        for index in range(TREE_MOST):
            opening = jnp.where(segs[index] == pars[index], segs[index], -1.0)
            if block + index < TREE_MOST - 1:
                opening = jnp.where(me > 0, opening, -1.0)
            first = jnp.maximum(first, opening)
        root = jnp.broadcast_to(jnp.max(first, axis=1, keepdims=True), (BLK, BLK))
        own_seg = jnp.broadcast_to(segs[-1], (BLK, BLK)).T
        own_par = jnp.broadcast_to(pars[-1], (BLK, BLK)).T
        for index in range(TREE_MOST):
            other = jnp.broadcast_to(segs[index], (BLK, BLK))
            allowed = (other == own_seg) | (other == own_par) | (other == root)
            if index == TREE_MOST - 1:
                allowed = allowed & later
            bias[path * BLOCKS + block, :, index * BLK : (index + 1) * BLK] = jnp.where(
                allowed, 0.0, NEG
            )

    scale = math.log2(math.e) / math.sqrt(HEAD)

    def attend(path, step, members):
        block, head, rows, _ = place_of(step)
        window = pl.ds(pl.multiple_of(block * BLK, BLK), SPAN)
        lanes = pl.ds(pl.multiple_of(head * HEAD, HEAD), HEAD)
        key = kbuf[path, window, lanes]
        value = vbuf[path, window, lanes]
        mask = bias[path * BLOCKS + block]
        parts = [
            pl.ds(pl.multiple_of(head * WIDE + member * HEAD, HEAD), HEAD) for member in members
        ]
        query = jnp.concatenate([qbuf[path, rows, part] for part in parts], axis=0)
        scores = lax.dot_general(
            query, key, (((1,), (1,)), ((), ())), preferred_element_type=jnp.float32
        )
        weights, totals = [], []
        for index in range(len(members)):
            score = scores[index * BLK : (index + 1) * BLK] * scale + mask
            weight = jnp.exp2(score - jnp.max(score, axis=1, keepdims=True))
            totals.append(jnp.sum(weight, axis=1, keepdims=True))
            weights.append(weight.astype(jnp.bfloat16))
        mixed = jnp.dot(
            jnp.concatenate(weights, axis=0), value, preferred_element_type=jnp.float32
        )
        for index, part in enumerate(parts):
            result = mixed[index * BLK : (index + 1) * BLK] / totals[index]
            stage[path, rows, part] = result.astype(jnp.bfloat16)

    def region(step, members):
        _, head, rows, _ = place_of(step)
        if members is None:
            return rows, slice(None)
        start = pl.multiple_of(head * WIDE + members[0] * HEAD, HEAD)
        return rows, pl.ds(start, len(members) * HEAD)

    def away(path, step, members):
        rows, columns = region(step, members)
        target, landed, to = (
            (forward, land_forward, up) if path == 0 else (returned, land_returned, down)
        )
        return pltpu.make_async_remote_copy(
            src_ref=stage.at[path, rows, columns],
            dst_ref=target.at[rows, columns],
            send_sem=send.at[path, step],
            recv_sem=landed.at[step],
            device_id=(to, me),
            device_id_type=MESH,
        )

    def stay(path, step, members):
        rows, columns = region(step, members)
        target, landed = (
            (returned, land_returned) if path == 0 else (forward, land_forward)
        )
        return pltpu.make_async_copy(
            stage.at[path, rows, columns], target.at[rows, columns], landed.at[step]
        )

    edges = (n_pipe - 1, 0)
    every = tuple(range(GROUP))

    def leave(path, step, members):
        @pl.when(place != edges[path])
        def _():
            away(path, step, members).start()

        @pl.when(place == edges[path])
        def _():
            stay(path, step, members).start()

    def fetch(step):
        @pl.when(step + AHEAD < STEPS)
        def _():
            query_copy(step + AHEAD).start()

        query_copy(step).wait()

    def work(step):
        fetch(step)
        for path in range(2):
            attend(path, step, every)

            @pl.when(step < KV_HEADS)
            def _():
                leave(path, step, every)

            @pl.when((step >= KV_HEADS) & (lax.rem(step, KV_HEADS) == KV_HEADS - 1))
            def _():
                leave(path, step, None)

    barrier = pltpu.get_barrier_semaphore()
    for target, met in (((up, me), place < n_pipe - 1), ((down, me), place > 0)):

        @pl.when(met)
        def _():
            pl.semaphore_signal(barrier, inc=1, device_id=target, device_id_type=MESH)

    pl.semaphore_signal(barrier, inc=1, device_id=(place, before), device_id_type=MESH)
    own_copy(0, 0).start()
    query_copy(0).start()
    for copy in infos:
        copy.start()
    own_copy(1, 0).start()
    own_copy(0, 0).wait()
    query_copy(0).wait()
    for copy in infos:
        copy.wait()
    own_copy(1, 0).wait()
    for path in range(2):
        build_bias(path, TREE_MOST - 1)
    for members in ((0,), (1,), (2, 3), (4, 5, 6, 7)):
        for path in range(2):
            attend(path, 0, members)
        if members == (0,):
            pl.semaphore_wait(barrier, jnp.where((place > 0) & (place < n_pipe - 1), 3, 2))
        for path in range(2):
            leave(path, 0, members)
        if members == (0,):
            for head in range(1, KV_HEADS):
                own_copy(0, head).start()
                own_copy(1, head).start()
            for step in range(1, AHEAD + 1):
                query_copy(step).start()
    for copy in halo:
        copy.start()
    for head in range(1, KV_HEADS):
        own_copy(0, head).wait()
        own_copy(1, head).wait()
    pl.loop(1, KV_HEADS)(work)
    for block in range(TREE_MOST, BLOCKS):
        for path in range(2):
            build_bias(path, block)
    half = (BLOCKS - TREE_MOST + 1) * KV_HEADS
    pl.loop(KV_HEADS, half)(work)
    for copy in halo:
        copy.wait()
    for block in range(TREE_MOST - 1):
        for path in range(2):
            build_bias(path, block)
    pl.loop(half, STEPS)(work)

    def settle(step, members):
        for path in range(2):

            @pl.when(place != edges[path])
            def _():
                away(path, step, members).wait_send()

            @pl.when(place != edges[1 - path])
            def _():
                away(path, step, members).wait_recv()

            @pl.when(place == edges[path])
            def _():
                stay(path, step, members).wait()

    @pl.loop(0, KV_HEADS)
    def _(step):
        settle(step, every)

    @pl.loop(1, BLOCKS)
    def _(block):
        settle(block * KV_HEADS + KV_HEADS - 1, None)


def flush(forward, returned, forward_out, returned_out, sem):
    copies = []
    for source, target in ((forward, forward_out), (returned, returned_out)):
        for index in range(PIECES):
            rows = pl.ds(index * (ROWS // PIECES), ROWS // PIECES)
            copies.append(
                pltpu.make_async_copy(source.at[rows], target.at[rows], sem.at[len(copies)])
            )
    for copy in copies:
        copy.start()
    for copy in copies:
        copy.wait()


def on_device(queries, keys, values, segment, parent, tree_lengths):
    width = KV_HEADS * GROUP * HEAD
    narrow = KV_HEADS * HEAD
    out = jax.ShapeDtypeStruct((ROWS, width), jnp.bfloat16)
    forward, returned = pl.pallas_call(
        kernel,
        out_shape=(out, out),
        in_specs=[pl.BlockSpec(memory_space=pltpu.HBM)] * 5,
        out_specs=[pl.BlockSpec(memory_space=pl.ANY)] * 2,
        scratch_shapes=[
            pltpu.VMEM((2, ROWS, width), jnp.bfloat16),
            pltpu.VMEM((2, REACH + ROWS, narrow), jnp.bfloat16),
            pltpu.VMEM((2, REACH + ROWS, narrow), jnp.bfloat16),
            pltpu.VMEM((2, REACH + ROWS), jnp.int32),
            pltpu.VMEM((2, REACH + ROWS), jnp.int32),
            pltpu.VMEM((2 * BLOCKS, BLK, SPAN), jnp.float32),
            pltpu.VMEM((2, ROWS, width), jnp.bfloat16),
            pltpu.SemaphoreType.DMA((STEPS,)),
            pltpu.SemaphoreType.DMA((2,)),
            pltpu.SemaphoreType.DMA((2, KV_HEADS)),
            pltpu.SemaphoreType.DMA((4,)),
            pltpu.SemaphoreType.DMA((4,)),
            pltpu.SemaphoreType.DMA((2, STEPS)),
            pltpu.SemaphoreType.DMA((STEPS,)),
            pltpu.SemaphoreType.DMA((STEPS,)),
        ],
        compiler_params=pltpu.CompilerParams(
            collective_id=0, has_side_effects=True, vmem_limit_bytes=40 << 20
        ),
        name="relay",
    )(*[pltpu.with_memory_space_constraint(x[0], pltpu.HBM) for x in (queries, keys, values, segment, parent)])
    anywhere = [pl.BlockSpec(memory_space=pl.ANY)] * 2
    forward, returned = pl.pallas_call(
        flush,
        out_shape=(out, out),
        in_specs=anywhere,
        out_specs=anywhere,
        scratch_shapes=[pltpu.SemaphoreType.DMA((2 * PIECES,))],
        compiler_params=pltpu.CompilerParams(vmem_limit_bytes=1 << 20),
        name="flush",
    )(forward, returned)
    return (forward[None], returned[None])


def solution(mesh):
    return jax.shard_map(
        on_device,
        mesh=mesh,
        in_specs=(
            P("pipe", None, "dp", None),
            P("pipe", None, "dp", None),
            P("pipe", None, "dp", None),
            P("pipe", None, "dp"),
            P("pipe", None, "dp"),
            P("pipe", None, None),
        ),
        out_specs=(P("pipe", "dp", None), P("pipe", "dp", None)),
        check_vma=False,
    )
```
